32 devices in a mesh: row: 4 (over z), col: 8 (over y, x, core).
Axes of the slice: x: 2, y: 2, z: 4, core: 2. Of those that a mesh axis runs over, the one named last changes fastest.
Arguments:
- scene_tokens: bfloat16 [64, 512, 180], P('row', 'col'), may hold values from -8 to 8
- block_qkv: bfloat16 [3, 180, 540], replicated, may hold values from -1.8 to 1.8
- block_proj: bfloat16 [3, 180, 180], replicated, may hold values from -0.4375 to 0.4375
- conv_squeeze: bfloat16 [3, 9, 180, 60], replicated, may hold values from -0.15625 to 0.15625
- conv_expand: bfloat16 [3, 9, 60, 180], replicated, may hold values from -0.25 to 0.25
- gate_down: bfloat16 [3, 180, 6], replicated, may hold values from -4 to 4
- gate_up: bfloat16 [3, 6, 180], replicated, may hold values from -6 to 6
- mlp_in: bfloat16 [4, 180, 360], replicated, may hold values from -0.4375 to 0.4375
- mlp_out: bfloat16 [4, 360, 180], replicated, may hold values from -0.3125 to 0.3125
- ocab_qkv: bfloat16 [180, 540], replicated, may hold values from -1.8 to 1.8
- ocab_proj: bfloat16 [180, 180], replicated, may hold values from -0.4375 to 0.4375
Outputs:
- refined: bfloat16 [64, 512, 180], P('row', 'col')
The draws below stay inside these ranges and needn't reach their ends.
All inputs are finite; a program needn't handle non-finite values.
Results may differ from the reference program's by a relative error of at most 0.034.
Values may be sent and summed in bfloat16 or wider, within the bound.
No kernel may reach another device: no remote copies, remote signals or barrier semaphores. Data moves between devices by JAX's collectives and lax.ppermute only.
A program may use at most 128 MiB of HBM per device.

```python
import math
import jax
import jax.numpy as jnp
from jax import lax

C = 180
HEADS = 6
WIN = 16
HID = 360
CC = 60
CS = 6
SHIFT = 8
OVL = 4
NH = 64
NW = 512


def draw_attention(key, layers_count):
    drawn = jax.random.normal(jax.random.fold_in(key, 11), (layers_count, C, 3 * C), jnp.float32) * C ** (-0.5)
    drawn = jnp.clip(drawn, -6.0 * C ** (-0.5), 6.0 * C ** (-0.5))
    return drawn


def draw_block_qkv(key, part):
    return draw_attention(key, 3).astype(jnp.bfloat16)


def draw_ocab_qkv(key, part):
    return draw_attention(key, 1)[0].astype(jnp.bfloat16)


def draw_scene_tokens(key, part):
    row_place = jnp.arange(NH, dtype=jnp.float32) / NH
    col_place = jnp.arange(NW, dtype=jnp.float32) / NW
    low_end, high_end = (math.log(0.6), math.log(1.6))
    region = jnp.exp(jax.random.uniform(jax.random.fold_in(key, 22), (NH // WIN, NW // WIN), jnp.float32, low_end, high_end))
    region = jnp.repeat(jnp.repeat(region, WIN, axis=0), WIN, axis=1)
    pattern = jnp.clip(jax.random.normal(jax.random.fold_in(key, 21), (C,), jnp.float32), -3.0, 3.0)
    noise = jnp.clip(jax.random.normal(jax.random.fold_in(key, 24), (NH, NW, C), jnp.float32), -4.0, 4.0)
    ramp = 0.1 * jnp.power(12.0, row_place)[:, None] * jnp.power(2.5, col_place)[None, :]
    drawn = noise + (ramp * region)[:, :, None] * pattern[None, None, :]
    return jnp.clip(drawn, -8.0, 8.0).astype(jnp.bfloat16)


def scatter_about(own_key, shape, scale, most, held_as=jnp.bfloat16):
    values = scale * jax.random.normal(own_key, shape, jnp.float32)
    return jnp.clip(values, min=-most, max=most).astype(held_as)


def setup_inputs(seed: int = 0) -> dict:
    key_of = jax.random.split(jax.random.key(seed), 12)
    scene_tokens = draw_scene_tokens(jax.random.fold_in(key_of[11], 71), 0)
    block_qkv = draw_block_qkv(jax.random.fold_in(key_of[11], 71), 0)
    block_proj = scatter_about(key_of[2], (3, C, C), C ** -0.5, 0.4375)
    conv_squeeze = scatter_about(key_of[3], (3, 9, C, CC), (9 * C) ** -0.5, 0.15625)
    conv_expand = scatter_about(key_of[4], (3, 9, CC, C), (9 * CC) ** -0.5, 0.25)
    gate_down = scatter_about(key_of[5], (3, C, CS), 1.0, 4.0)
    gate_up = scatter_about(key_of[6], (3, CS, C), 1.0, 6.0)
    mlp_in = scatter_about(key_of[7], (4, C, HID), C ** -0.5, 0.4375)
    mlp_out = scatter_about(key_of[8], (4, HID, C), HID ** -0.5, 0.3125)
    ocab_qkv = draw_ocab_qkv(jax.random.fold_in(key_of[11], 71), 0)
    ocab_proj = scatter_about(key_of[10], (C, C), C ** -0.5, 0.4375)
    return dict(scene_tokens=scene_tokens, block_qkv=block_qkv, block_proj=block_proj, conv_squeeze=conv_squeeze, conv_expand=conv_expand, gate_down=gate_down, gate_up=gate_up, mlp_in=mlp_in, mlp_out=mlp_out, ocab_qkv=ocab_qkv, ocab_proj=ocab_proj)


EPSILON = 1e-05
MASKED = -1000000000.0

def layer_norm(stream):
    middle = lax.optimization_barrier(jnp.mean(stream, axis=-1, keepdims=True))
    centered = stream - middle
    spread = lax.optimization_barrier(jnp.mean(centered * centered, axis=-1, keepdims=True))
    return (centered * lax.rsqrt(spread + EPSILON)).astype(jnp.bfloat16)

def partition(field):
    height, breadth, channels = field.shape
    blocks = field.reshape(height // WIN, WIN, breadth // WIN, WIN, channels)
    return blocks.transpose(0, 2, 1, 3, 4).reshape(height // WIN, breadth // WIN, WIN * WIN, channels)

def assemble(blocks):
    row_count, col_count, window_cells, channels = blocks.shape
    field = blocks.reshape(row_count, col_count, WIN, WIN, channels).transpose(0, 2, 1, 3, 4)
    return field.reshape(row_count * WIN, col_count * WIN, channels)

def attend_windows(queries, keys, values, allowed, proj_weight):
    groups, length, channels = queries.shape
    head_size = channels // HEADS
    split_q = queries.reshape(groups, length, HEADS, head_size).astype(jnp.float32)
    split_k = keys.reshape(groups, keys.shape[1], HEADS, head_size).astype(jnp.float32)
    split_v = values.reshape(groups, values.shape[1], HEADS, head_size).astype(jnp.float32)
    scores = jnp.einsum('gqhd,gkhd->ghqk', split_q, split_k) * head_size ** (-0.5)
    if allowed is not None:
        scores = jnp.where(allowed[:, None], scores, MASKED)
    highest = lax.optimization_barrier(jnp.max(scores, axis=-1, keepdims=True))
    powers = jnp.exp(scores - highest)
    weights = (powers / lax.optimization_barrier(jnp.sum(powers, axis=-1, keepdims=True))).astype(jnp.bfloat16)
    heads_out = jnp.einsum('ghqk,gkhd->gqhd', weights.astype(jnp.float32), split_v).astype(jnp.bfloat16)
    merged = heads_out.reshape(groups * length, channels)
    return jnp.dot(merged, proj_weight, preferred_element_type=jnp.float32).reshape(groups, length, channels)

def rolled_labels(start, number, extent):
    position = start + jnp.arange(number, dtype=jnp.int32)
    return jnp.where(position >= extent - SHIFT, 2, jnp.where(position >= extent - WIN, 1, 0))

def window_branch(normed, qkv_weight, proj_weight, shifted):
    projected = jnp.dot(normed.reshape(NH * NW, C), qkv_weight, preferred_element_type=jnp.float32)
    projected = projected.astype(jnp.bfloat16).reshape(NH, NW, 3 * C)
    if shifted:
        projected = jnp.roll(projected, (-SHIFT, -SHIFT), axis=(0, 1))
    windows = partition(projected)
    column_labels = rolled_labels(0, NW, NW).reshape(NW // WIN, 1, WIN)

    def one_row(pair):
        row_windows, number = pair
        allowed = None
        if shifted:
            row_labels = rolled_labels(number * WIN, WIN, NH)
            labels = (3 * row_labels[None, :, None] + column_labels).reshape(NW // WIN, WIN * WIN)
            allowed = labels[:, :, None] == labels[:, None, :]
        return attend_windows(row_windows[..., :C], row_windows[..., C:2 * C], row_windows[..., 2 * C:], allowed, proj_weight)
    result = assemble(lax.map(one_row, (windows, jnp.arange(NH // WIN, dtype=jnp.int32))))
    if shifted:
        result = jnp.roll(result, (SHIFT, SHIFT), axis=(0, 1))
    return result

def convolve(extended, taps, height, breadth):
    channels_in = extended.shape[2]
    summed = jnp.zeros((height * breadth, taps.shape[2]), jnp.float32)
    for offset in range(9):
        row_step, col_step = (offset // 3, offset % 3)
        window = extended[row_step:row_step + height, col_step:col_step + breadth].reshape(height * breadth, channels_in)
        summed = summed + jnp.dot(window, taps[offset], preferred_element_type=jnp.float32)
    return summed.reshape(height, breadth, taps.shape[2])

def channel_gate(expanded, squeeze_weight, excite_weight):
    pooled = lax.optimization_barrier(jnp.sum(expanded, axis=(0, 1))) / (NH * NW)
    squeezed = jax.nn.relu(jnp.dot(pooled[None], squeeze_weight.astype(jnp.float32), precision=lax.Precision.HIGHEST))
    scaled = jax.nn.sigmoid(jnp.dot(squeezed, excite_weight.astype(jnp.float32), precision=lax.Precision.HIGHEST))
    return expanded * scaled[0]

def feed_forward(normed, in_weight, out_weight):
    height, breadth = (normed.shape[0], normed.shape[1])
    hidden = jax.nn.gelu(jnp.dot(normed.reshape(height * breadth, C), in_weight, preferred_element_type=jnp.float32), approximate=False).astype(jnp.bfloat16)
    return jnp.dot(hidden, out_weight, preferred_element_type=jnp.float32).reshape(height, breadth, C)

def intersection_branch(normed, qkv_weight, proj_weight):
    tokens_flat = normed.reshape(NH * NW, C)
    queries = jnp.dot(tokens_flat, qkv_weight[:, :C], preferred_element_type=jnp.float32).astype(jnp.bfloat16).reshape(NH, NW, C)
    key_values = jnp.dot(tokens_flat, qkv_weight[:, C:], preferred_element_type=jnp.float32).astype(jnp.bfloat16).reshape(NH, NW, 2 * C)
    key_values = jnp.pad(key_values, ((OVL, OVL), (OVL, OVL), (0, 0)))
    context_side = WIN + 2 * OVL
    starts = jnp.arange(NW // WIN, dtype=jnp.int32) * WIN

    def one_row(pair):
        row_queries, number = pair
        band_rows = lax.dynamic_slice_in_dim(key_values, number * WIN, context_side, 0)
        context = jax.vmap(lambda column_start: lax.dynamic_slice_in_dim(band_rows, column_start, context_side, 1))(starts)
        context = context.reshape(NW // WIN, context_side * context_side, 2 * C)
        return attend_windows(row_queries, context[..., :C], context[..., C:], None, proj_weight)
    result = lax.map(one_row, (partition(queries), jnp.arange(NH // WIN, dtype=jnp.int32)))
    return assemble(result)

def reference(scene_tokens, block_qkv, block_proj, conv_squeeze, conv_expand, gate_down, gate_up, mlp_in, mlp_out, ocab_qkv, ocab_proj):
    stream = scene_tokens.astype(jnp.float32)
    edges = ((1, 1), (1, 1), (0, 0))
    for block_number in range(3):
        normed = layer_norm(stream)
        attended = window_branch(normed, block_qkv[block_number], block_proj[block_number], block_number == 1)
        hidden = jax.nn.gelu(convolve(jnp.pad(normed, edges), conv_squeeze[block_number], NH, NW), approximate=False).astype(jnp.bfloat16)
        expanded = convolve(jnp.pad(hidden, edges), conv_expand[block_number], NH, NW)
        gated = channel_gate(expanded, gate_down[block_number], gate_up[block_number])
        stream = stream + attended + gated
        stream = stream + feed_forward(layer_norm(stream), mlp_in[block_number], mlp_out[block_number])
    stream = stream + intersection_branch(layer_norm(stream), ocab_qkv, ocab_proj)
    stream = stream + feed_forward(layer_norm(stream), mlp_in[3], mlp_out[3])
    return stream.astype(jnp.bfloat16)
```

```python
import functools

import jax
import jax.numpy as jnp
from jax import lax
from jax.experimental import pallas as pl
from jax.experimental.pallas import tpu as pltpu
from jax.sharding import PartitionSpec as P

C = 180
HEADS = 6
HEAD = 30
WIN = 16
HID = 360
CC = 60
CP = 64
SHIFT = 8
OVL = 4
EDGE = 8
EPSILON = 1e-05
MASKED = -1000000000.0
BF16 = jnp.bfloat16
F32 = jnp.float32


def dot(a, b):
    return jnp.dot(a, b, preferred_element_type=F32)


def dot_nt(a, b):
    return lax.dot_general(a, b, (((1,), (1,)), ((), ())), preferred_element_type=F32)


def layer_norm(x):
    middle = jnp.sum(x, axis=-1, keepdims=True) * (1.0 / C)
    centered = x - middle
    spread = jnp.sum(centered * centered, axis=-1, keepdims=True) * (1.0 / C)
    return (centered * lax.rsqrt(spread + EPSILON)).astype(BF16)


def gelu(v):
    return v * (lax.erf(v * (0.5**0.5)) + 1.0) * 0.5


def head_masks(rows):
    lane = lax.broadcasted_iota(jnp.int32, (rows, C), 1)
    return [(lane >= HEAD * h) & (lane < HEAD * (h + 1)) for h in range(HEADS)]


def attend(q, k, v, bias):
    n, m = q.shape[0], k.shape[0]
    q_masks = head_masks(n)
    v_masks = head_masks(m)
    zero_q = jnp.zeros_like(q)
    zero_v = jnp.zeros_like(v)
    one_v = jnp.ones_like(v)
    top = jnp.zeros((n, C), F32)
    bottom = jnp.zeros((n, C), F32)
    for h in range(HEADS):
        scores = dot_nt(jnp.where(q_masks[h], q, zero_q), k) * HEAD ** (-0.5)
        if bias is not None:
            scores = scores + bias
        highest = jnp.max(scores, axis=-1, keepdims=True)
        powers = jnp.exp(scores - highest).astype(BF16)
        top = top + dot(powers, jnp.where(v_masks[h], v, zero_v))
        bottom = bottom + dot(powers, jnp.where(v_masks[h], one_v, zero_v))
    return (top / bottom).astype(BF16)


def norm_kernel(x_ref, u_ref):
    u_ref[...] = layer_norm(x_ref[...].astype(F32))


def window_kernel(u_ref, qkv_ref, proj_ref, out_ref):
    w = qkv_ref[...]
    wq, wk, wv = w[:, :C], w[:, C : 2 * C], w[:, 2 * C :]
    proj = proj_ref[...]
    height, breadth = u_ref.shape[0], u_ref.shape[1]
    for i in range(height // WIN):

        def body(j, carry):
            cols = pl.ds(pl.multiple_of(j * WIN, WIN), WIN)
            rows = pl.ds(i * WIN, WIN)
            u = u_ref[rows, cols, :].reshape(WIN * WIN, C)
            q = dot(u, wq).astype(BF16)
            k = dot(u, wk).astype(BF16)
            v = dot(u, wv).astype(BF16)
            heads = attend(q, k, v, None)
            out_ref[rows, cols, :] = dot(heads, proj).reshape(WIN, WIN, C)
            return carry

        lax.fori_loop(0, breadth // WIN, body, 0)


def place(ext, flags_ref, u_ref, row_e, row_o, col_e, col_o, width, left, convert):
    height, breadth = u_ref.shape[0], u_ref.shape[1]
    row_odd = flags_ref[0] == 1
    col_odd = flags_ref[1] == 1
    inside = [flags_ref[2 + s] == 1 for s in range(4)]

    def pick(cond, a, b, keep):
        value = jnp.where(cond, a[...].astype(F32), b[...].astype(F32))
        return convert(jnp.where(keep, value, 0.0))

    ext[width : width + height, left : left + breadth, :] = convert(u_ref[...].astype(F32))
    ext[0:width, left : left + breadth, :] = pick(row_odd, row_e, row_o, inside[0])
    ext[width + height :, left : left + breadth, :] = pick(row_odd, row_o, row_e, inside[1])
    tall = height + 2 * width
    west = pick(col_odd, col_e, col_o, inside[2])
    east = pick(col_odd, col_o, col_e, inside[3])
    rows_at = lax.broadcasted_iota(jnp.int32, (tall, 1, 1), 0)
    real = ((rows_at >= width) | inside[0]) & ((rows_at < width + height) | inside[1])
    west = jnp.where(real, west.astype(F32), 0.0).astype(west.dtype)
    east = jnp.where(real, east.astype(F32), 0.0).astype(east.dtype)
    side = col_e.shape[1]
    ext[0:tall, left - side : left, :] = west
    ext[0:tall, left + breadth : left + breadth + side, :] = east


def shifted_kernel(
    flags_ref, u_ref, row_e, row_o, col_e, col_o, qkv_ref, proj_ref, out_ref, ext, wide
):
    height, breadth = u_ref.shape[0], u_ref.shape[1]
    place(ext, flags_ref, u_ref, row_e, row_o, col_e, col_o, SHIFT, SHIFT, lambda x: x)
    w = qkv_ref[...]
    wq, wk, wv = w[:, :C], w[:, C : 2 * C], w[:, 2 * C :]
    proj = proj_ref[...]
    north, south, west, east = [flags_ref[2 + s] == 1 for s in range(4)]
    count_i = height // WIN + 1
    count_j = breadth // WIN + 1
    key = lax.broadcasted_iota(jnp.int32, (1, WIN * WIN), 1)
    key_row, key_col = key // WIN, key % WIN
    for i in range(count_i):
        low = SHIFT if i == 0 else 0
        high = SHIFT if i == count_i - 1 else WIN

        def body(j, carry):
            cols = pl.ds(pl.multiple_of(j * WIN, WIN), WIN)
            u = ext[i * WIN : (i + 1) * WIN, cols, :]
            part = u[low:high].reshape((high - low) * WIN, C).astype(BF16)
            u = u.reshape(WIN * WIN, C).astype(BF16)
            bad = jnp.zeros((1, WIN * WIN), jnp.bool_)
            if i == 0:
                bad = bad | ((key_row < SHIFT) & jnp.logical_not(north))
            if i == count_i - 1:
                bad = bad | ((key_row >= SHIFT) & jnp.logical_not(south))
            bad = bad | ((key_col < SHIFT) & (jnp.logical_not(west) & (j == 0)))
            bad = bad | ((key_col >= SHIFT) & (jnp.logical_not(east) & (j == count_j - 1)))
            bias = jnp.where(bad, MASKED, 0.0)
            q = dot(part, wq).astype(BF16)
            k = dot(u, wk).astype(BF16)
            v = dot(u, wv).astype(BF16)
            heads = attend(q, k, v, bias)
            wide[i * WIN + low - SHIFT : i * WIN + high - SHIFT, cols, :] = dot(
                heads, proj
            ).reshape(high - low, WIN, C)
            return carry

        lax.fori_loop(0, count_j, body, 0)
    out_ref[...] = wide[:, SHIFT : SHIFT + breadth, :]


def cross_kernel(
    flags_ref, u_ref, row_e, row_o, col_e, col_o, qkv_ref, proj_ref, out_ref, ext, keys, values
):
    height, breadth = u_ref.shape[0], u_ref.shape[1]
    place(ext, flags_ref, u_ref, row_e, row_o, col_e, col_o, OVL, EDGE, lambda x: x)
    w = qkv_ref[...]
    wq, wk, wv = w[:, :C], w[:, C : 2 * C], w[:, 2 * C :]
    proj = proj_ref[...]
    tall, long = ext.shape[0], ext.shape[1]
    side = WIN + 2 * OVL
    flat = pltpu.roll(ext[...].reshape(tall * long, C), tall * long - (EDGE - OVL), 0)
    flat = flat.astype(BF16)
    keys[...] = dot(flat, wk).astype(BF16).astype(F32).reshape(tall, long, C)
    values[...] = dot(flat, wv).astype(BF16).astype(F32).reshape(tall, long, C)
    for i in range(height // WIN):

        def body(j, carry):
            at = j * WIN
            rows = pl.ds(i * WIN, WIN)
            u = u_ref[rows, pl.ds(at, WIN), :].reshape(WIN * WIN, C)
            q = dot(u, wq).astype(BF16)
            area = (pl.ds(i * WIN, side), pl.ds(at, side), slice(None))
            k = keys[area].reshape(side * side, C).astype(BF16)
            v = values[area].reshape(side * side, C).astype(BF16)
            heads = attend(q, k, v, None)
            out_ref[rows, pl.ds(at, WIN), :] = dot(heads, proj).reshape(WIN, WIN, C)
            return carry

        for j in range(breadth // WIN):
            body(j, 0)


def conv_kernel(
    width, flags_ref, u_ref, row_e, row_o, col_e, col_o, w1_ref, w2_ref, out_ref, sum_ref, ext, hid
):
    height, breadth = u_ref.shape[0], u_ref.shape[1]
    pitch = breadth + 2 * EDGE
    grid = ext.at[...]
    place(grid, flags_ref, u_ref, row_e, row_o, col_e, col_o, width, EDGE, lambda x: x)
    north, south, west, east = [flags_ref[2 + s] == 1 for s in range(4)]
    tall = height + 4
    first = width - 2
    flat = ext[first : first + tall].reshape(tall * pitch, C)
    acc = None
    for b in range(3):
        moved = flat if b == 1 else pltpu.roll(flat, (1 - b) % (tall * pitch), 0)
        part = dot(moved.astype(BF16), w1_ref[b])
        acc = part if acc is None else acc + part
    acc = acc.reshape(tall, pitch, 3 * CP)
    rows = height + 2
    pre = (
        acc[0:rows, :, 0:CP]
        + acc[1 : rows + 1, :, CP : 2 * CP]
        + acc[2 : rows + 2, :, 2 * CP : 3 * CP]
    )
    hidden = gelu(pre)
    row_at = lax.broadcasted_iota(jnp.int32, (rows, pitch, CP), 0)
    col_at = lax.broadcasted_iota(jnp.int32, (rows, pitch, CP), 1)
    real = ((row_at >= 1) | north) & ((row_at < rows - 1) | south)
    real = real & (col_at >= jnp.where(west, EDGE - 1, EDGE))
    real = real & (col_at < EDGE + breadth + jnp.where(east, 1, 0))
    hidden = jnp.where(real, hidden, 0.0).reshape(rows * pitch, CP)
    total = rows * pitch
    three = jnp.concatenate(
        [
            pltpu.roll(hidden, 1, 0),
            hidden,
            pltpu.roll(hidden, total - 1, 0),
        ],
        axis=1,
    ).astype(BF16)
    out = None
    for a in range(3):
        part = dot(three[a * pitch : (a + height) * pitch], w2_ref[a])
        out = part if out is None else out + part
    out = out.reshape(height, pitch, C)[:, EDGE : EDGE + breadth, :]
    out_ref[...] = out
    sums = jnp.sum(jnp.sum(out, axis=0), axis=0, keepdims=True)
    for i in range(sum_ref.shape[0]):
        sum_ref[i] = sums


def ff_tail(x, in_ref, out_w_ref):
    hidden = gelu(dot(layer_norm(x), in_ref[...])).astype(BF16)
    return x + dot(hidden, out_w_ref[...])


def block_kernel(
    rim, area, flags_ref, x_ref, att_ref, exp_ref, sums_ref, down_ref, up_ref, in_ref, out_w_ref,
    y_ref, u_ref, even_ref, odd_ref,
):
    pooled = jnp.sum(sums_ref[...], axis=0) * (1.0 / area)
    squeezed = jnp.sum(down_ref[...] * pooled, axis=-1, keepdims=True)
    squeezed = jnp.maximum(squeezed, 0.0)
    gate = jax.nn.sigmoid(jnp.sum(up_ref[...] * squeezed, axis=0, keepdims=True))
    height, breadth = x_ref.shape[0], x_ref.shape[1]
    step = 4

    def body(r, carry):
        rows = pl.ds(r * step, step)
        x = x_ref[rows].reshape(step * breadth, C).astype(F32)
        x = x + att_ref[rows].reshape(step * breadth, C)
        x = x + exp_ref[rows].reshape(step * breadth, C) * gate
        y = ff_tail(x, in_ref, out_w_ref)
        y_ref[rows] = y.reshape(step, breadth, C)
        u_ref[rows] = layer_norm(y).reshape(step, breadth, C)
        return carry

    lax.fori_loop(0, height // step, body, 0)
    rims(rim, flags_ref, u_ref, even_ref, odd_ref)


def rims(rim, flags_ref, u_ref, even_ref, odd_ref):
    height = u_ref.shape[0]
    head = u_ref[0:rim]
    tail = u_ref[height - rim :]
    odd = flags_ref[0] == 1

    @pl.when(odd)
    def _():
        even_ref[...] = head
        odd_ref[...] = tail

    @pl.when(jnp.logical_not(odd))
    def _():
        even_ref[...] = tail
        odd_ref[...] = head


def first_kernel(rim, flags_ref, x_ref, u_ref, even_ref, odd_ref):
    u_ref[...] = layer_norm(x_ref[...].astype(F32))
    rims(rim, flags_ref, u_ref, even_ref, odd_ref)


def last_kernel(x_ref, att_ref, in_ref, out_w_ref, y_ref):
    height, breadth = x_ref.shape[0], x_ref.shape[1]
    step = 4

    def body(r, carry):
        rows = pl.ds(r * step, step)
        x = (x_ref[rows] + att_ref[rows]).reshape(step * breadth, C)
        y = ff_tail(x, in_ref, out_w_ref)
        y_ref[rows] = y.astype(BF16).reshape(step, breadth, C)
        return carry

    lax.fori_loop(0, height // step, body, 0)


VM = pl.BlockSpec(memory_space=pltpu.VMEM)
SM = pl.BlockSpec(memory_space=pltpu.SMEM)


def call(kernel, name, outs, scratch, flags, *args):
    specs = [VM] * len(args)
    if flags is not None:
        specs = [SM] + specs
        args = (flags,) + args
    return pl.pallas_call(
        kernel,
        out_shape=outs,
        in_specs=specs,
        out_specs=jax.tree.map(lambda _: VM, outs),
        scratch_shapes=scratch,
        name=name,
        compiler_params=pltpu.CompilerParams(vmem_limit_bytes=48 * 1024 * 1024),
    )(*args)


def swap(value, axis, odd):
    count = lax.axis_size(axis)
    pairs = []
    for i in range(count):
        step = 1 if (i % 2 == 0) != odd else -1
        pairs.append((i, (i + step) % count))
    return lax.ppermute(value, axis, pairs)


def exchange(u, even, odd, width, side, flags):
    row_e = swap(even, "row", False)
    row_o = swap(odd, "row", True)
    row_odd = flags[0] == 1
    col_odd = flags[1] == 1
    above = jnp.where(row_odd, row_e, row_o)
    below = jnp.where(row_odd, row_o, row_e)
    breadth = u.shape[1]
    head = jnp.concatenate([a[:, :side] for a in (above, u, below)], axis=0)
    tail = jnp.concatenate([a[:, breadth - side :] for a in (above, u, below)], axis=0)
    col_e = swap(jnp.where(col_odd, head, tail), "col", False)
    col_o = swap(jnp.where(col_odd, tail, head), "col", True)
    return row_e, row_o, col_e, col_o


def local(
    scene_tokens, block_qkv, block_proj, conv_squeeze, conv_expand, gate_down, gate_up,
    mlp_in, mlp_out, ocab_qkv, ocab_proj,
):
    height, breadth = scene_tokens.shape[0], scene_tokens.shape[1]
    row_count, col_count = lax.axis_size("row"), lax.axis_size("col")
    area = height * row_count * breadth * col_count
    devices = row_count * col_count
    row, col = lax.axis_index("row"), lax.axis_index("col")
    flags = jnp.stack(
        [
            row % 2,
            col % 2,
            (row > 0).astype(jnp.int32),
            (row < row_count - 1).astype(jnp.int32),
            (col > 0).astype(jnp.int32),
            (col < col_count - 1).astype(jnp.int32),
        ]
    ).astype(jnp.int32)
    w1 = conv_squeeze.reshape(3, 3, 3, C, CC).transpose(0, 2, 3, 1, 4)
    w1 = jnp.pad(w1, ((0, 0), (0, 0), (0, 0), (0, 0), (0, CP - CC))).reshape(3, 3, C, 3 * CP)
    w2 = jnp.pad(conv_expand, ((0, 0), (0, 0), (0, CP - CC), (0, 0))).reshape(3, 3, 3 * CP, C)
    down = gate_down.transpose(0, 2, 1).astype(F32)
    up = gate_up.astype(F32)

    def shape(rows, cols, dtype):
        return jax.ShapeDtypeStruct((rows, cols, C), dtype)

    tile = shape(height, breadth, F32)
    tile16 = shape(height, breadth, BF16)
    widths = [2, SHIFT, 2, OVL]

    def rim_shape(k):
        return shape(widths[k], breadth, BF16)

    u, even, odd = call(
        functools.partial(first_kernel, widths[0]), "norm",
        (tile16, rim_shape(0), rim_shape(0)), [], flags, scene_tokens,
    )
    stream = scene_tokens
    for k in range(3):
        width = widths[k]
        halo = exchange(u, even, odd, width, width, flags)
        if k == 1:
            tall, long = height + 2 * SHIFT, breadth + 2 * SHIFT
            att = call(
                shifted_kernel, "shifted_attention", tile,
                [pltpu.VMEM((tall, long, C), F32), pltpu.VMEM((height, long, C), F32)],
                flags, u, *halo, block_qkv[k], block_proj[k],
            )
        else:
            att = call(window_kernel, "window_attention", tile, [], None, u, block_qkv[k], block_proj[k])
        pitch = breadth + 2 * EDGE
        expanded, sums = call(
            functools.partial(conv_kernel, width), "convolutions",
            (tile, jax.ShapeDtypeStruct((devices, 1, C), F32)),
            [pltpu.VMEM((height + 2 * width, pitch, C), F32), pltpu.VMEM((8, 128), F32)],
            flags, u, *halo, w1[k], w2[k],
        )
        sums = lax.all_to_all(sums, ("row", "col"), 0, 0)
        stream, u, even, odd = call(
            functools.partial(block_kernel, widths[k + 1], area), "feed_forward",
            (tile, tile16, rim_shape(k + 1), rim_shape(k + 1)), [],
            flags, stream, att, expanded, sums, down[k], up[k], mlp_in[k], mlp_out[k],
        )
    halo = exchange(u, even, odd, OVL, EDGE, flags)
    tall, long = height + 2 * OVL, breadth + 2 * EDGE
    att = call(
        cross_kernel, "cross_attention", tile,
        [pltpu.VMEM((tall, long, C), F32)] * 3,
        flags, u, *halo, ocab_qkv, ocab_proj,
    )
    return call(last_kernel, "last", tile16, [], None, stream, att, mlp_in[3], mlp_out[3])


def solution(mesh):
    return jax.shard_map(
        local,
        mesh=mesh,
        in_specs=(P("row", "col", None),) + (P(),) * 10,
        out_specs=P("row", "col", None),
        check_vma=False,
    )
```

```python
import functools
import math

import jax
import jax.numpy as jnp
from jax import lax
from jax.experimental import pallas as pl
from jax.experimental.pallas import tpu as pltpu
from jax.sharding import PartitionSpec as P

C = 180
HEADS = 6
HEAD = 30
WIN = 16
HID = 360
CC = 60
CP = 64
SHIFT = 8
OVL = 4
EDGE = 8
EPSILON = 1e-05
MASKED = -1000000000.0
BF16 = jnp.bfloat16
F32 = jnp.float32


def dot(a, b):
    return jnp.dot(a, b, preferred_element_type=F32)


def dot_nt(a, b):
    return lax.dot_general(a, b, (((1,), (1,)), ((), ())), preferred_element_type=F32)


def layer_norm(x):
    middle = jnp.sum(x, axis=-1, keepdims=True) * (1.0 / C)
    centered = x - middle
    spread = jnp.sum(centered * centered, axis=-1, keepdims=True) * (1.0 / C)
    return (centered * lax.rsqrt(spread + EPSILON)).astype(BF16)


def gelu(v):
    return v * (lax.erf(v * (0.5**0.5)) + 1.0) * 0.5


LANES = 256
SCALE = HEAD ** (-0.5) * math.log2(math.e)


def head_masks(rows, lanes):
    lane = lax.broadcasted_iota(jnp.int32, (rows, lanes), 1)
    return [(lane >= HEAD * h) & (lane < HEAD * (h + 1)) for h in range(HEADS)]


def attend(q, k, v, bias):
    n = q.shape[0]
    zero = jnp.zeros_like(q)
    stack = jnp.concatenate([jnp.where(mask, q, zero) for mask in head_masks(n, C)], axis=0)
    scores = dot_nt(stack, k)
    if bias is not None:
        scores = scores + bias
    highest = jnp.max(scores, axis=-1, keepdims=True)
    powers = jnp.exp2((scores - highest) * SCALE).astype(BF16)
    mixed = dot(powers, v)
    share = 1.0 / mixed[:, C : C + 1]
    mixed = mixed[:, :C] * share
    out = mixed[:n]
    for h, mask in enumerate(head_masks(n, C)):
        if h:
            out = jnp.where(mask, mixed[h * n : (h + 1) * n], out)
    return out.astype(BF16)


def split_qkv(w):
    wv = jnp.concatenate([w[:, 2 * C :], jnp.zeros((C, LANES - C), w.dtype)], axis=1)
    return w[:, :C], w[:, C : 2 * C], wv


def with_ones(v):
    lane = lax.broadcasted_iota(jnp.int32, v.shape, 1)
    return jnp.where(lane >= C, 1.0, v)


def norm_kernel(x_ref, u_ref):
    u_ref[...] = layer_norm(x_ref[...].astype(F32))


def window_kernel(k_at, start, count, u_ref, qkv_ref, proj_ref, after_ref, out_ref):
    wq, wk, wv = split_qkv(qkv_ref[k_at])
    proj = proj_ref[k_at]
    for i in range(u_ref.shape[0] // WIN):

        def body(j, carry):
            cols = pl.ds(pl.multiple_of((j + start) * WIN, WIN), WIN)
            rows = pl.ds(i * WIN, WIN)
            u = u_ref[rows, cols, :].reshape(WIN * WIN, C)
            q = dot(u, wq).astype(BF16)
            k = dot(u, wk).astype(BF16)
            v = with_ones(dot(u, wv)).astype(BF16)
            heads = attend(q, k, v, None)
            out_ref[rows, pl.ds(pl.multiple_of(j * WIN, WIN), WIN), :] = dot(
                heads, proj
            ).reshape(WIN, WIN, C)
            return carry

        lax.fori_loop(0, count, body, 0)


def place(ext, flags_ref, u_ref, row_e, row_o, col_e, col_o, width, left, convert):
    height, breadth = u_ref.shape[0], u_ref.shape[1]
    row_odd = flags_ref[0] == 1
    col_odd = flags_ref[1] == 1
    inside = [flags_ref[2 + s] == 1 for s in range(4)]

    def pick(cond, a, b, keep):
        value = jnp.where(cond, a[...].astype(F32), b[...].astype(F32))
        return convert(jnp.where(keep, value, 0.0))

    ext[width : width + height, left : left + breadth, :] = u_ref[...].astype(F32)
    ext[0:width, left : left + breadth, :] = pick(row_odd, row_e, row_o, inside[0])
    ext[width + height :, left : left + breadth, :] = pick(row_odd, row_o, row_e, inside[1])
    tall = height + 2 * width
    west = pick(col_odd, col_e, col_o, inside[2])
    east = pick(col_odd, col_o, col_e, inside[3])
    rows_at = lax.broadcasted_iota(jnp.int32, (tall, 1, 1), 0)
    real = ((rows_at >= width) | inside[0]) & ((rows_at < width + height) | inside[1])
    west = jnp.where(real, west.astype(F32), 0.0).astype(west.dtype)
    east = jnp.where(real, east.astype(F32), 0.0).astype(east.dtype)
    side = col_e.shape[1]
    ext[0:tall, left - side : left, :] = west
    ext[0:tall, left + breadth : left + breadth + side, :] = east


def shifted_kernel(
    k_at, i, flags_ref, u_ref, row_e, row_o, col_e, col_o, qkv_ref, proj_ref, after_ref, out_ref,
    ext, wide,
):
    height, breadth = u_ref.shape[0], u_ref.shape[1]
    place(ext, flags_ref, u_ref, row_e, row_o, col_e, col_o, SHIFT, SHIFT, lambda x: x)
    wq, wk, wv = split_qkv(qkv_ref[k_at])
    proj = proj_ref[k_at]
    north, south, west, east = [flags_ref[2 + s] == 1 for s in range(4)]
    count_i = height // WIN + 1
    count_j = breadth // WIN + 1
    key = lax.broadcasted_iota(jnp.int32, (1, WIN * WIN), 1)
    key_row, key_col = key // WIN, key % WIN
    low = SHIFT if i == 0 else 0
    high = SHIFT if i == count_i - 1 else WIN

    def body(j, carry):
        cols = pl.ds(pl.multiple_of(j * WIN, WIN), WIN)
        u = ext[i * WIN : (i + 1) * WIN, cols, :]
        part = u[low:high].reshape((high - low) * WIN, C).astype(BF16)
        u = u.reshape(WIN * WIN, C).astype(BF16)
        bad = jnp.zeros((1, WIN * WIN), jnp.bool_)
        if i == 0:
            bad = bad | ((key_row < SHIFT) & jnp.logical_not(north))
        if i == count_i - 1:
            bad = bad | ((key_row >= SHIFT) & jnp.logical_not(south))
        bad = bad | ((key_col < SHIFT) & (jnp.logical_not(west) & (j == 0)))
        bad = bad | ((key_col >= SHIFT) & (jnp.logical_not(east) & (j == count_j - 1)))
        bias = jnp.where(bad, MASKED, 0.0)
        q = dot(part, wq).astype(BF16)
        k = dot(u, wk).astype(BF16)
        v = with_ones(dot(u, wv)).astype(BF16)
        heads = attend(q, k, v, bias)
        wide[:, cols, :] = dot(heads, proj).reshape(high - low, WIN, C)
        return carry

    lax.fori_loop(0, count_j, body, 0)
    out_ref[...] = wide[:, SHIFT : SHIFT + breadth, :]


def cross_kernel(
    k_at, flags_ref, u_ref, row_e, row_o, col_e, col_o, qkv_ref, proj_ref, out_ref, ext, keys, values
):
    height, breadth = u_ref.shape[0], u_ref.shape[1]
    place(ext, flags_ref, u_ref, row_e, row_o, col_e, col_o, OVL, EDGE, lambda x: x)
    wq, wk, wv = split_qkv(qkv_ref[k_at] if len(qkv_ref.shape) == 3 else qkv_ref[...])
    proj = proj_ref[k_at] if len(proj_ref.shape) == 3 else proj_ref[...]
    tall, long = ext.shape[0], ext.shape[1]
    side = WIN + 2 * OVL
    flat = pltpu.roll(ext[...].reshape(tall * long, C), tall * long - (EDGE - OVL), 0)
    flat = flat.astype(BF16)
    keys[...] = dot(flat, wk).astype(BF16).astype(F32).reshape(tall, long, C)
    values[...] = with_ones(dot(flat, wv)).astype(BF16).astype(F32).reshape(tall, long, LANES)
    for i in range(height // WIN):

        def body(j, carry):
            at = j * WIN
            rows = pl.ds(i * WIN, WIN)
            u = u_ref[rows, pl.ds(at, WIN), :].reshape(WIN * WIN, C)
            q = dot(u, wq).astype(BF16)
            area = (pl.ds(i * WIN, side), pl.ds(at, side), slice(None))
            k = keys[area].reshape(side * side, C).astype(BF16)
            v = values[area].reshape(side * side, LANES).astype(BF16)
            heads = attend(q, k, v, None)
            out_ref[rows, pl.ds(at, WIN), :] = dot(heads, proj).reshape(WIN, WIN, C)
            return carry

        for j in range(breadth // WIN):
            body(j, 0)


def three_taps(ref, k_at, taps):
    pad = jnp.zeros((CP - CC, C), BF16)
    parts = []
    for t in taps:
        parts += [ref[k_at, t], pad]
    return jnp.concatenate(parts, axis=0)


def squeeze_kernel(
    k_at, width, raw, flags_ref, u_ref, row_e, row_o, col_e, col_o, w1_ref, w2_ref, after_ref,
    three_ref, sum_ref, ext,
):
    height, breadth = u_ref.shape[0], u_ref.shape[1]
    pitch = breadth + 2 * EDGE
    convert = (lambda x: layer_norm(x).astype(F32)) if raw else (lambda x: x)
    place(ext, flags_ref, u_ref, row_e, row_o, col_e, col_o, width, EDGE, convert)
    north, south, west, east = [flags_ref[2 + s] == 1 for s in range(4)]
    tall = height + 4
    first = width - 2
    flat = ext[first : first + tall].reshape(tall * pitch, C)
    acc = None
    for b in range(3):
        moved = flat if b == 1 else pltpu.roll(flat, (1 - b) % (tall * pitch), 0)
        part = dot_nt(moved.astype(BF16), three_taps(w1_ref, k_at, (b, 3 + b, 6 + b)))
        acc = part if acc is None else acc + part
    acc = acc.reshape(tall, pitch, 3 * CP)
    rows = height + 2
    pre = (
        acc[0:rows, :, 0:CP]
        + acc[1 : rows + 1, :, CP : 2 * CP]
        + acc[2 : rows + 2, :, 2 * CP : 3 * CP]
    )
    hidden = gelu(pre)
    row_at = lax.broadcasted_iota(jnp.int32, (rows, pitch, CP), 0)
    col_at = lax.broadcasted_iota(jnp.int32, (rows, pitch, CP), 1)
    real = ((row_at >= 1) | north) & ((row_at < rows - 1) | south)
    real = real & (col_at >= jnp.where(west, EDGE - 1, EDGE))
    real = real & (col_at < EDGE + breadth + jnp.where(east, 1, 0))
    hidden = jnp.where(real, hidden, 0.0).astype(BF16).astype(F32).reshape(rows * pitch, CP)
    total = rows * pitch
    three = jnp.concatenate(
        [pltpu.roll(hidden, 1, 0), hidden, pltpu.roll(hidden, total - 1, 0)], axis=1
    )
    three_ref[...] = three.astype(BF16)
    lines = jnp.sum(three.reshape(rows, pitch, 3 * CP)[:, EDGE : EDGE + breadth, :], axis=1)
    sums = jnp.zeros((1, C), F32)
    for a in range(3):
        box = jnp.sum(lines[a : a + height], axis=0, keepdims=True)
        high = box.astype(BF16)
        rest = box - high.astype(F32)
        middle = rest.astype(BF16)
        low = (rest - middle.astype(F32)).astype(BF16)
        taps = three_taps(w2_ref, k_at, (3 * a, 3 * a + 1, 3 * a + 2))
        for piece in (high, middle, low):
            wide = jnp.broadcast_to(piece.astype(F32), (16, 3 * CP)).astype(BF16)
            sums = sums + dot(wide, taps)[0:1]
    sum_ref[...] = sums


def expand_kernel(k_at, three_ref, w2_ref, after_ref, out_ref):
    height, breadth = out_ref.shape[0], out_ref.shape[1]
    pitch = breadth + 2 * EDGE
    out = None
    for a in range(3):
        part = dot(
            three_ref[a * pitch : (a + height) * pitch, :],
            three_taps(w2_ref, k_at, (3 * a, 3 * a + 1, 3 * a + 2)),
        )
        out = part if out is None else out + part
    out_ref[...] = out.reshape(height, pitch, C)[:, EDGE : EDGE + breadth, :]


def ff_tail(k_at, x, in_ref, out_w_ref):
    hidden = gelu(dot(layer_norm(x), in_ref[k_at])).astype(BF16)
    return x + dot(hidden, out_w_ref[k_at])


def block_kernel(
    k_at, rim, area, pieces, by_rows, flags_ref, x_ref, exp_ref, sums_ref, down_ref, up_ref, in_ref,
    out_w_ref, *refs,
):
    att_refs = refs[:pieces]
    y_ref, u_ref = refs[pieces : pieces + 2]
    rim_refs = refs[pieces + 2 :]
    pooled = sums_ref[...] * (1.0 / area)
    squeezed = jnp.sum(down_ref[k_at].astype(F32) * pooled, axis=-1, keepdims=True)
    squeezed = jnp.maximum(squeezed, 0.0)
    gate = jax.nn.sigmoid(jnp.sum(up_ref[k_at].astype(F32) * squeezed, axis=0, keepdims=True))
    height, breadth = x_ref.shape[0], x_ref.shape[1]
    step = 4

    def chunk(rows, att):
        x = x_ref[rows].reshape(step * breadth, C).astype(F32)
        x = x + att.reshape(step * breadth, C)
        x = x + exp_ref[rows].reshape(step * breadth, C) * gate
        y = ff_tail(k_at, x, in_ref, out_w_ref)
        y_ref[rows] = y.reshape(step, breadth, C)
        u_ref[rows] = layer_norm(y).reshape(step, breadth, C)

    if by_rows:
        part = height // pieces
        for p in range(pieces):

            def body(r, carry):
                chunk(pl.ds(p * part + r * step, step), att_refs[p][pl.ds(r * step, step)])
                return carry

            lax.fori_loop(0, part // step, body, 0)
    else:

        def body(r, carry):
            rows = pl.ds(r * step, step)
            chunk(rows, jnp.concatenate([ref[rows] for ref in att_refs], axis=1))
            return carry

        lax.fori_loop(0, height // step, body, 0)
    for index, width in enumerate(rim):
        rims(width, flags_ref, u_ref, rim_refs[2 * index], rim_refs[2 * index + 1])


def rims(rim, flags_ref, u_ref, even_ref, odd_ref):
    height = u_ref.shape[0]
    head = u_ref[0:rim]
    tail = u_ref[height - rim :]
    odd = flags_ref[0] == 1

    @pl.when(odd)
    def _():
        even_ref[...] = head
        odd_ref[...] = tail

    @pl.when(jnp.logical_not(odd))
    def _():
        even_ref[...] = tail
        odd_ref[...] = head


def first_kernel(x_ref, u_ref):
    u_ref[...] = layer_norm(x_ref[...].astype(F32))


def last_kernel(k_at, x_ref, att_ref, in_ref, out_w_ref, y_ref):
    height, breadth = x_ref.shape[0], x_ref.shape[1]
    step = 4

    def body(r, carry):
        rows = pl.ds(r * step, step)
        x = (x_ref[rows] + att_ref[rows]).reshape(step * breadth, C)
        y = ff_tail(k_at, x, in_ref, out_w_ref)
        y_ref[rows] = y.astype(BF16).reshape(step, breadth, C)
        return carry

    lax.fori_loop(0, height // step, body, 0)


VM = pl.BlockSpec(memory_space=pltpu.VMEM)
SM = pl.BlockSpec(memory_space=pltpu.SMEM)
ANY = pl.BlockSpec(memory_space=pl.ANY)


def call(kernel, name, outs, scratch, flags, *args, after=None, limit=20):
    specs = [VM] * len(args)
    if flags is not None:
        specs = [SM] + specs
        args = (flags,) + args
    if after is not None:
        specs = specs + [ANY]
        args = args + (after,)
    return pl.pallas_call(
        kernel,
        out_shape=outs,
        in_specs=specs,
        out_specs=jax.tree.map(lambda _: VM, outs),
        scratch_shapes=scratch,
        name=name,
        compiler_params=pltpu.CompilerParams(vmem_limit_bytes=limit * 1024 * 1024),
    )(*args)


def swap(value, axis, odd, ring=True):
    count = lax.axis_size(axis)
    pairs = []
    for i in range(count):
        other = i + (1 if (i % 2 == 0) != odd else -1)
        if ring or 0 <= other < count:
            pairs.append((i, other % count))
    return lax.ppermute(value, axis, pairs)


def groups_of(count, first):
    bits = [1 << b for b in range(count.bit_length() - 1)]
    groups = [[b] for b in bits[:first]]
    rest = bits[first:]
    return groups + [rest[i : i + 2] for i in range(0, len(rest), 2)]


def all_sum_steps():
    steps = []
    for axis, first in (("col", 1), ("row", 0)):
        count = lax.axis_size(axis)
        for group in groups_of(count, first):
            masks = [group[0]] if len(group) == 1 else [group[0], group[1], group[0] + group[1]]
            steps.append((axis, count, masks))
    return steps


def sum_step(value, step):
    axis, count, masks = step
    got = [lax.ppermute(value, axis, [(i, i ^ m) for i in range(count)]) for m in masks]
    return functools.reduce(jnp.add, got, value)


def exchange_rows(even, odd, ring):
    return swap(even, "row", False), swap(odd, "row", True, ring)


def exchange_cols(u, row_e, row_o, side, flags):
    row_odd = flags[0] == 1
    col_odd = flags[1] == 1
    above = jnp.where(row_odd, row_e, row_o)
    below = jnp.where(row_odd, row_o, row_e)
    breadth = u.shape[1]
    head = jnp.concatenate([a[:, :side] for a in (above, u, below)], axis=0)
    tail = jnp.concatenate([a[:, breadth - side :] for a in (above, u, below)], axis=0)
    col_e = swap(jnp.where(col_odd, head, tail), "col", False)
    col_o = swap(jnp.where(col_odd, tail, head), "col", True)
    return col_e, col_o


def local(
    scene_tokens, block_qkv, block_proj, conv_squeeze, conv_expand, gate_down, gate_up,
    mlp_in, mlp_out, ocab_qkv, ocab_proj,
):
    height, breadth = scene_tokens.shape[0], scene_tokens.shape[1]
    row_count, col_count = lax.axis_size("row"), lax.axis_size("col")
    area = height * row_count * breadth * col_count
    row, col = lax.axis_index("row"), lax.axis_index("col")
    flags = jnp.stack(
        [
            row % 2,
            col % 2,
            (row > 0).astype(jnp.int32),
            (row < row_count - 1).astype(jnp.int32),
            (col > 0).astype(jnp.int32),
            (col < col_count - 1).astype(jnp.int32),
        ]
    ).astype(jnp.int32)
    w1 = conv_squeeze.swapaxes(2, 3)
    down = gate_down.swapaxes(1, 2)

    def shape(rows, cols, dtype):
        return jax.ShapeDtypeStruct((rows, cols, C), dtype)

    tile = shape(height, breadth, F32)
    tile16 = shape(height, breadth, BF16)
    pitch = breadth + 2 * EDGE
    hidden_shape = jax.ShapeDtypeStruct(((height + 2) * pitch, 3 * CP), BF16)
    narrow = 2
    windows = breadth // WIN
    half, quarter = windows // 2, windows // 4
    cuts = [(0, half), (half, quarter), (half + quarter, windows - half - quarter)]

    def rim_shapes(widths):
        return sum(((shape(w, breadth, BF16),) * 2 for w in widths), ())

    def window_piece(k, u, piece, after):
        start, count = cuts[piece]
        return call(
            functools.partial(window_kernel, k, start, count), "window_attention",
            shape(height, count * WIN, F32), [], None, u, block_qkv, block_proj, after=after,
        )

    def squeeze(k, u, rows, cols, after):
        return call(
            functools.partial(squeeze_kernel, k, narrow, k == 0), "squeeze",
            (hidden_shape, jax.ShapeDtypeStruct((1, C), F32)),
            [pltpu.VMEM((height + 2 * narrow, pitch, C), F32)],
            flags, u, *rows, *cols, w1, conv_expand, after=after,
        )

    def expand(k, three, after):
        return call(
            functools.partial(expand_kernel, k), "expand", tile, [], None, three, conv_expand,
            after=after,
        )

    row_odd = flags[0] == 1
    head, tail = scene_tokens[:narrow], scene_tokens[height - narrow :]
    even, odd = jnp.where(row_odd, head, tail), jnp.where(row_odd, tail, head)
    source = scene_tokens
    stream = scene_tokens
    u = call(first_kernel, "norm", tile16, [], None, scene_tokens)
    rim = [even, odd]
    steps = all_sum_steps()
    for k in range(3):
        rows = exchange_rows(rim[0], rim[1], True)
        if k == 1:
            rows8 = exchange_rows(rim[2], rim[3], False)
            cols = exchange_cols(u, *rows, narrow, flags)
            three, sums = squeeze(k, u, rows, cols, u)
            sums = sum_step(sums, steps[0])
            expanded = expand(k, three, sums)
            cols8 = exchange_cols(u, *rows8, SHIFT, flags)
            tall, long = height + 2 * SHIFT, breadth + 2 * SHIFT
            pieces = []
            for i in range(height // WIN + 1):
                if i < len(steps) - 1:
                    sums = sum_step(sums, steps[1 + i])
                pieces.append(
                    call(
                        functools.partial(shifted_kernel, k, i), "shifted_attention",
                        shape(WIN // 2, breadth, F32),
                        [pltpu.VMEM((tall, long, C), F32), pltpu.VMEM((WIN // 2, long, C), F32)],
                        flags, u, *rows8, *cols8, block_qkv, block_proj,
                        after=pieces[-1] if pieces else expanded,
                    )
                )
            for step in steps[1 + height // WIN + 1 :]:
                sums = sum_step(sums, step)
            by_rows = True
        else:
            first = window_piece(k, u, 0, u)
            cols = exchange_cols(source, *rows, narrow, flags)
            second = window_piece(k, u, 1, first)
            three, sums = squeeze(k, u, rows, cols, second)
            sums = sum_step(sums, steps[0])
            expanded = expand(k, three, sums)
            third = window_piece(k, u, 2, expanded)
            for step in steps[1:]:
                sums = sum_step(sums, step)
            pieces = [first, second, third]
            by_rows = False
        widths = {0: [narrow, SHIFT], 1: [narrow], 2: [OVL]}[k]
        stream, u, *rim = call(
            functools.partial(block_kernel, k, widths, area, len(pieces), by_rows), "feed_forward",
            (tile, tile16) + rim_shapes(widths), [],
            flags, stream, expanded, sums, down, gate_up, mlp_in, mlp_out, *pieces,
        )
        source = u
    rows = exchange_rows(*rim, True)
    cols = exchange_cols(u, *rows, EDGE, flags)
    tall, long = height + 2 * OVL, breadth + 2 * EDGE
    att = call(
        functools.partial(cross_kernel, 0), "cross_attention", tile,
        [pltpu.VMEM((tall, long, C), F32)] * 2 + [pltpu.VMEM((tall, long, LANES), F32)],
        flags, u, *rows, *cols, ocab_qkv, ocab_proj,
    )
    return call(
        functools.partial(last_kernel, 3), "last", tile16, [], None, stream, att, mlp_in, mlp_out
    )


def solution(mesh):
    return jax.shard_map(
        local,
        mesh=mesh,
        in_specs=(P("row", "col", None),) + (P(),) * 10,
        out_specs=P("row", "col", None),
        check_vma=False,
    )
```
